128 devices in a mesh: grp: 8 (over x, core), exp: 16 (over z, y).
Axes of the slice: x: 4, y: 4, z: 4, core: 2. Of those that a mesh axis runs over, the one named last changes fastest.
Arguments:
- tokens: bfloat16 [16384, 4096], P(('grp', 'exp')), may hold values from -6 to 6
- expert_ids: int32 [16384, 8], P(('grp', 'exp')), may hold values from 0 to 15, all different within a row; in each aligned block of 128 rows (0 to 127, 128 to 255, ...) at most 80 rows name the same one
- gate_fixed: int32 [16384, 8], P(('grp', 'exp')), may hold values from 1 to 65535
- w_gate: bfloat16 [16, 4096, 768], P('exp', None, 'grp'), may hold values from -0.09375 to 0.09375
- w_up: bfloat16 [16, 4096, 768], P('exp', None, 'grp'), may hold values from -0.09375 to 0.09375
- w_down: bfloat16 [16, 768, 4096], P('exp', 'grp'), may hold values from -0.21875 to 0.21875
Outputs:
- mixed: bfloat16 [16384, 4096], P(('grp', 'exp'))
The draws below stay inside these ranges and needn't reach their ends.
Inputs may be any that keep to these rules, and one draw needn't show every extreme that they name: `expert_ids`: each row names 8 different experts. Among the rows of one device no expert is named by more than 80 rows, and in every draw some expert is named by exactly 80 rows of some device.
All inputs are finite; a program needn't handle non-finite values.
Results may differ from the reference program's by a relative error of at most 0.0058.
Values may be sent and summed in bfloat16 or wider, within the bound.
No kernel may reach another device: no remote copies, remote signals or barrier semaphores. Data moves between devices by JAX's collectives and lax.ppermute only.
A program may use at most 128 MiB of HBM per device.

```python
import math
import jax
import jax.numpy as jnp
import numpy as np
from jax import lax

D = 4096
FF = 768
EXPERTS = 16
TOPK = 8
TOK_DEV = 128
CAP = 80
TOKENS = 16384
DEVICES = 128


def touch_ends(values, stream_key, low, top_value):
    shape = values.shape
    index_at = [jax.random.randint(jax.random.fold_in(stream_key, axis), (), 0, shape[axis]) for axis in range(len(shape))]
    values = values.at[tuple(index_at)].set(low)
    longest = shape.index(max(shape))
    index_at[longest] = (index_at[longest] + 1) % shape[longest]
    return values.at[tuple(index_at)].set(top_value)


def steps_of(key, shape, cuts, low, high):
    def one(position, blocks):
        draws = jax.random.uniform(jax.random.fold_in(jax.random.fold_in(key, 6), position), (blocks,), jnp.float32, low / len(cuts), high / len(cuts))
        return jnp.repeat(jnp.exp(draws), shape[position] // blocks).reshape((-1,) + (1,) * (len(shape) - position - 1))

    factor_of = one(*cuts[0])
    for cut in cuts[1:]:
        factor_of = factor_of * one(*cut)
    return factor_of


def shared_out(own_key, own, number, rows, number_of, top, limit, lean):
    order = jax.random.permutation(own_key, number_of)
    crowded, ordinary = portions_of(number_of, rows * top, limit, lean, True), portions_of(number_of, rows * top, limit, lean, False)
    places = jnp.arange(number_of)

    def named(tallies, rotation):
        used = int((tallies > 0).sum())
        fixed = max(1, used // 4)
        passed = fixed + (places - fixed + rotation * (used - fixed)) % max(1, number_of - fixed)
        return jnp.zeros((number_of,), jnp.int32).at[order[jnp.where(places < fixed, places, passed)]].set(jnp.asarray(tallies, jnp.int32))

    tallies = jnp.where(number % 4 == 0, named(crowded, number // 4), named(ordinary, number - number // 4 - 1))
    mixed = jax.random.permutation(jax.random.fold_in(own, 3), number_of)
    giver, receiver = mixed[0:number_of // 2 * 2:2], mixed[1:number_of // 2 * 2:2]
    slack = jnp.minimum(tallies[giver] - 1, limit - tallies[receiver]) // 2
    slack = jnp.where((giver == order[0]) | (receiver == order[0]) | (tallies[receiver] == 0), 0, jnp.maximum(slack, 0))
    passed = jax.random.randint(jax.random.fold_in(own, 4), (number_of // 2,), 0, 1 << 20) % (slack + 1)
    tallies = tallies.at[giver].add(-passed).at[receiver].add(passed)
    members = jnp.searchsorted(jnp.cumsum(tallies), jnp.arange(rows * top), side="right").astype(jnp.int32)
    table = members.reshape(top, rows).T
    table = table[jax.random.permutation(jax.random.fold_in(own, 1), rows)]
    rotation = jax.random.randint(jax.random.fold_in(own, 2), (rows, 1), 0, top)
    return jnp.take_along_axis(table, (jnp.arange(top)[None, :] + rotation) % top, axis=1)


def portions_of(count, total, reach, skew, full):
    loads = [(1 << 20) // math.isqrt(rank ** skew) + 1 for rank in range(1, count + 1)]
    largest = reach if full else min(reach, max(-(-total // count), total * loads[0] // sum(loads)))
    least = 1 if total - largest >= count - 1 else 0
    given, rest = [largest] + [least] * (count - 1), total - largest - least * (count - 1)
    while rest > 0:
        candidates = [i for i in range(1, count) if given[i] < largest] or [i for i in range(1, count) if given[i] < reach]
        mass, left = sum([loads[i] for i in candidates]), rest
        for i in candidates:
            extra = min(reach - given[i], max(1, left * loads[i] // mass), rest)
            given[i] = given[i] + extra
            rest = rest - extra
    return np.array(given)


def scatter_about(stream_key, shape, deviation, most, cuts=(), kind=jnp.bfloat16):
    result = deviation * jax.random.normal(stream_key, shape, jnp.float32)
    if cuts:
        result = result * steps_of(stream_key, shape, cuts, -0.22, 0.18)
    return jnp.clip(result, -most, most).astype(kind)


def setup_inputs(seed: int = 0) -> dict:
    splits = jax.random.split(jax.random.key(seed), 7)
    tokens = scatter_about(splits[0], (TOKENS, D), 1.0, 6.0, ((0, 128),))
    expert_ids_keys = jax.random.split(jax.random.fold_in(splits[1], 1), TOKENS // TOK_DEV)
    expert_ids_turns = jax.random.permutation(jax.random.fold_in(splits[1], 3), TOKENS // TOK_DEV)
    expert_ids = jax.vmap(lambda own, number: shared_out(jax.random.fold_in(splits[1], 2), own, number, TOK_DEV, EXPERTS, TOPK, CAP, 2))(expert_ids_keys, expert_ids_turns).reshape((TOKENS, TOPK))
    gate_fixed = touch_ends(jax.random.randint(splits[2], (TOKENS, TOPK), 1, 65536), jax.random.fold_in(splits[2], 1), 1, 65535).astype(jnp.int32)
    w_gate = scatter_about(splits[3], (EXPERTS, D, FF), D ** -0.5, 0.09375, ((0, 16), (2, 8)))
    w_up = scatter_about(splits[4], (EXPERTS, D, FF), D ** -0.5, 0.09375, ((0, 16), (2, 8)))
    w_down = scatter_about(splits[5], (EXPERTS, FF, D), FF ** -0.5, 0.21875, ((0, 16), (1, 8)))
    return {"tokens": tokens, "expert_ids": expert_ids, "gate_fixed": gate_fixed, "w_gate": w_gate, "w_up": w_up, "w_down": w_down}


def reference(tokens, expert_ids, gate_fixed, w_gate, w_up, w_down):
    most_rows = DEVICES * CAP
    weight = gate_fixed.astype(jnp.float32) / 65536.0

    def one_expert(total, expert):
        chosen = expert_ids == expert
        routed = jnp.any(chosen, axis=1)
        order = jnp.argsort((1 - routed.astype(jnp.int32)), stable=True).astype(jnp.int32)
        picked = order[:most_rows]
        rows = tokens[picked]
        gate_part = jnp.dot(rows, w_gate[expert], preferred_element_type=jnp.float32)
        up_part = jnp.dot(rows, w_up[expert], preferred_element_type=jnp.float32)
        hidden = (jax.nn.silu(gate_part) * up_part).astype(jnp.bfloat16)
        expert_out = jnp.dot(hidden, w_down[expert], preferred_element_type=jnp.float32).astype(jnp.bfloat16)
        token_weight = jnp.sum(jnp.where(chosen, weight, 0.0), axis=1)[picked]
        term = token_weight[:, None] * expert_out.astype(jnp.float32)
        return total.at[picked].add(term), None

    start = jnp.zeros(tokens.shape, jnp.float32)
    total, unused = lax.scan(one_expert, start, jnp.arange(EXPERTS, dtype=jnp.int32))
    return total.astype(jnp.bfloat16)
```

```python
import jax
import jax.numpy as jnp
from jax import lax
from jax.sharding import PartitionSpec as P

EXPERTS = 16
CAP = 80
META = 128


OFFS = [(dz, dy) for dz in (0, 1, -1, 2) for dy in (0, 1, -1, 2)]


def get_exp(x, dz, dy):
    pairs = [
        (((z + dz) % 4) * 4 + (y + dy) % 4, z * 4 + y) for z in range(4) for y in range(4)
    ]
    return lax.ppermute(x, "exp", pairs)


def put_exp(x, dz, dy):
    return get_exp(x, -dz, -dy)


def get_x(v, dx):
    pairs = [(((x + dx) % 4) * 2 + c, x * 2 + c) for x in range(4) for c in range(2)]
    return lax.ppermute(v, "grp", pairs)


def get_core(v):
    pairs = [(x * 2 + 1 - c, x * 2 + c) for x in range(4) for c in range(2)]
    return lax.ppermute(v, "grp", pairs)


def gather_weights(w):
    half = w.shape[0] // 2
    right = get_x(w, 1)
    left = get_x(w, -1)
    own_other = get_core(w)
    far_a = get_x(right[:half], 1)
    far_b = get_x(left[half:], -1)
    shards = [w, right, left, own_other, get_core(right), get_core(left)]
    far = jnp.concatenate([far_a, far_b], axis=0)
    return shards + [far, get_core(far)]


def gather_tokens(t):
    b = {(0, 0): t}
    for dz, dy in ((1, 0), (0, 1), (-1, 0), (0, -1)):
        b[dz, dy] = get_exp(t, dz, dy)
    b[1, 1] = get_exp(b[0, 1], 1, 0)
    b[1, -1] = get_exp(b[1, 0], 0, -1)
    b[-1, -1] = get_exp(b[0, -1], -1, 0)
    b[-1, 1] = get_exp(b[-1, 0], 0, 1)
    zz = [get_exp(b[1, 0][:64], 1, 0), get_exp(b[-1, 0][64:], -1, 0)]
    yy = [get_exp(b[0, 1][:64], 0, 1), get_exp(b[0, -1][64:], 0, -1)]
    b[2, 0] = jnp.concatenate(zz, axis=0)
    b[0, 2] = jnp.concatenate(yy, axis=0)
    b[2, 1] = get_exp(b[1, 1], 1, 0)
    b[2, -1] = get_exp(b[-1, -1], -1, 0)
    b[1, 2] = get_exp(b[1, 1], 0, 1)
    b[-1, 2] = get_exp(b[-1, -1], 0, -1)
    quarters = [
        get_exp(b[1, 2][0:32], 1, 0),
        get_exp(b[-1, 2][32:64], -1, 0),
        get_exp(b[2, 1][64:96], 0, 1),
        get_exp(b[2, -1][96:128], 0, -1),
    ]
    b[2, 2] = jnp.concatenate(quarters, axis=0)
    return b


def add(*terms):
    total = terms[0].astype(jnp.float32)
    for term in terms[1:]:
        total = total + term.astype(jnp.float32)
    return total.astype(jnp.bfloat16)


def rejoin(a, b):
    return jnp.concatenate([a, b], axis=0)


def reduce_back(p):
    far = p[2, 2]
    q0 = put_exp(far[0:32], 1, 0)
    q1 = put_exp(far[32:64], -1, 0)
    q2 = put_exp(far[64:96], 0, 1)
    q3 = put_exp(far[96:128], 0, -1)

    def with_rows(block, start, rows):
        stop = start + rows.shape[0]
        return jnp.concatenate(
            [block[:start], add(block[start:stop], rows), block[stop:]], axis=0
        )

    s12 = put_exp(with_rows(p[1, 2], 0, q0), 0, 1)
    sm12 = put_exp(with_rows(p[-1, 2], 32, q1), 0, -1)
    s21 = put_exp(with_rows(p[2, 1], 64, q2), 1, 0)
    s2m1 = put_exp(with_rows(p[2, -1], 96, q3), -1, 0)

    za = put_exp(p[2, 0][:64], 1, 0)
    zb = put_exp(p[2, 0][64:], -1, 0)
    ya = put_exp(p[0, 2][:64], 0, 1)
    yb = put_exp(p[0, 2][64:], 0, -1)
    s1m1 = put_exp(p[1, -1], 0, -1)
    sm11 = put_exp(p[-1, 1], 0, 1)
    s11 = put_exp(add(p[1, 1], s12, s21), 1, 0)
    sm1m1 = put_exp(add(p[-1, -1], sm12, s2m1), -1, 0)

    def near(block, whole, start, half):
        stop = start + 64
        parts = []
        for lo in (0, 64):
            terms = [block[lo : lo + 64], whole[lo : lo + 64]]
            if lo == start:
                terms.append(half)
            parts.append(add(*terms))
        return jnp.concatenate(parts, axis=0)

    n10 = put_exp(near(p[1, 0], s1m1, 0, za), 1, 0)
    nm10 = put_exp(near(p[-1, 0], sm11, 64, zb), -1, 0)
    n01 = put_exp(near(p[0, 1], s11, 0, ya), 0, 1)
    n0m1 = put_exp(near(p[0, -1], sm1m1, 64, yb), 0, -1)
    return add(p[0, 0], n10, nm10, n01, n0m1)


def expert_blocks(blocks, me, gate_t, up_t, down):
    width = down.shape[1]
    stacked = jnp.stack(blocks)
    rows, meta = stacked[:, :, :width], stacked[:, :, width:].astype(jnp.float32)
    mine = (jnp.arange(EXPERTS) == me).astype(jnp.float32)
    place = jnp.sum(meta[:, :, 0:16] * mine, axis=2)
    high = jnp.sum(meta[:, :, 16:32] * mine, axis=2)
    low = jnp.sum(meta[:, :, 32:48] * mine, axis=2)
    weight = (high * 256.0 + low) / 65536.0
    hit = place[:, None, :] == jnp.arange(1, CAP + 1, dtype=jnp.float32)[None, :, None]
    select = hit.astype(jnp.bfloat16)
    slot_weight = jnp.sum(jnp.where(hit, weight[:, None, :], 0.0), axis=2)
    x = jnp.einsum("bst,btd->bsd", select, rows, preferred_element_type=jnp.float32)
    x = x.astype(jnp.bfloat16).reshape(-1, width)
    contract = (((1,), (1,)), ((), ()))
    gate = lax.dot_general(x, gate_t, contract, preferred_element_type=jnp.float32)
    up = lax.dot_general(x, up_t, contract, preferred_element_type=jnp.float32)
    hidden = (jax.nn.silu(gate) * up).astype(jnp.bfloat16)
    out = jnp.dot(hidden, down, preferred_element_type=jnp.float32)
    out = (out * slot_weight.reshape(-1, 1)).astype(jnp.bfloat16).reshape(-1, CAP, width)
    part = jnp.einsum("bst,bsd->btd", select, out, preferred_element_type=jnp.float32)
    part = part.astype(jnp.bfloat16)
    return [part[i] for i in range(len(blocks))]


def per_device(tokens, expert_ids, gate_fixed, w_gate, w_up, w_down):
    me = lax.axis_index("exp")
    rows = tokens.shape[0]
    hit = expert_ids[:, :, None] == jnp.arange(EXPERTS, dtype=jnp.int32)
    routed = jnp.any(hit, axis=1).astype(jnp.int32)
    place = jnp.cumsum(routed, axis=0) * routed
    gate = jnp.sum(jnp.where(hit, gate_fixed[:, :, None], 0), axis=1)
    meta = jnp.concatenate(
        [place, gate // 256, gate % 256, jnp.zeros((rows, META - 48), jnp.int32)], axis=1
    ).astype(jnp.bfloat16)
    blocks = gather_tokens(jnp.concatenate([tokens, meta], axis=1))

    gate_t = jnp.concatenate(gather_weights(w_gate[0].T), axis=0)
    up_t = jnp.concatenate(gather_weights(w_up[0].T), axis=0)
    down = jnp.concatenate(gather_weights(w_down[0]), axis=0)

    batches = [
        [(2, 2), (1, 2), (-1, 2), (2, 1), (2, -1)],
        [(2, 0), (0, 2), (1, 1), (1, -1), (-1, 1), (-1, -1)],
        [(0, 0), (1, 0), (-1, 0), (0, 1), (0, -1)],
    ]
    partial = {}
    for batch in batches:
        outs = expert_blocks([blocks[o] for o in batch], me, gate_t, up_t, down)
        partial.update(zip(batch, outs))
    return reduce_back(partial)


def solution(mesh):
    in_specs = (
        P(("grp", "exp"), None),
        P(("grp", "exp"), None),
        P(("grp", "exp"), None),
        P("exp", None, "grp"),
        P("exp", None, "grp"),
        P("exp", "grp", None),
    )
    out_specs = P(("grp", "exp"), None)
    return jax.shard_map(
        per_device, mesh=mesh, in_specs=in_specs, out_specs=out_specs, check_vma=False
    )
```

```python
import functools

import jax
import jax.numpy as jnp
from jax import lax
from jax.experimental import pallas as pl
from jax.experimental.pallas import tpu as pltpu
from jax.sharding import PartitionSpec as P

EXPERTS = 16
CAP = 80
NTILE = 256
CTILE = 512


TREE = {
    (1, 0): ((1, 0), (0, 0)),
    (-1, 0): ((-1, 0), (0, 0)),
    (0, 1): ((0, 1), (0, 0)),
    (0, -1): ((0, -1), (0, 0)),
    (-1, -1): ((-1, 0), (0, -1)),
    (1, -1): ((0, -1), (1, 0)),
    (-1, 1): ((0, 1), (-1, 0)),
    (1, 1): ((1, 0), (0, 1)),
    (2, -1): ((-1, 0), (-1, -1)),
    (-1, 2): ((0, -1), (-1, -1)),
    (0, 2): ((0, 1), (0, 1)),
    (2, 0): ((1, 0), (1, 0)),
    (2, 2): ((0, -1), (2, -1)),
    (1, 2): ((0, 1), (1, 1)),
    (2, 1): ((1, 0), (1, 1)),
}

BATCHES = [
    [(0, 0), (1, 0), (-1, 0), (0, 1), (0, -1)],
    [(2, 2), (2, 1), (1, 2)],
    [(2, -1), (-1, 2), (2, 0), (0, 2)],
    [(-1, -1), (1, 1), (1, -1), (-1, 1)],
]


def get_exp(x, dz, dy):
    pairs = [
        (((z + dz) % 4) * 4 + (y + dy) % 4, z * 4 + y) for z in range(4) for y in range(4)
    ]
    return lax.ppermute(x, "exp", pairs)


def get_x(v, dx):
    pairs = [(((x + dx) % 4) * 2 + c, x * 2 + c) for x in range(4) for c in range(2)]
    return lax.ppermute(v, "grp", pairs)


def get_core(v):
    pairs = [(x * 2 + 1 - c, x * 2 + c) for x in range(4) for c in range(2)]
    return lax.ppermute(v, "grp", pairs)


def gather_weights(w):
    half = w.shape[0] // 2
    right = get_x(w, 1)
    left = get_x(w, -1)
    far_a = get_x(right[:half], 1)
    far_b = get_x(left[half:], -1)
    mine = [w, right, left, far_a, far_b]
    return mine + [get_core(v) for v in mine]


def gather_tokens(t):
    blocks = {(0, 0): t}
    for offset, (way, before) in TREE.items():
        blocks[offset] = get_exp(blocks[before], *way)
    return blocks


def reduce_back(partial):
    terms = {offset: [value] for offset, value in partial.items()}
    for offset, (way, before) in reversed(TREE.items()):
        own = terms[offset]
        value = own[0]
        if len(own) > 1:
            value = sum(v.astype(jnp.float32) for v in own).astype(jnp.bfloat16)
        terms[before].append(get_exp(value, -way[0], -way[1]))
    return sum(v.astype(jnp.float32) for v in terms[0, 0]).astype(jnp.bfloat16)


def weight_pieces(n):
    half = 3 * n // 2
    pieces = []
    for core in range(2):
        for k in range(3):
            for kind in range(3):
                pieces.append((core * 5 + k, kind * n, kind, (core * 4 + k) * n, n))
        for kind in range(3):
            lo, hi = kind * n, (kind + 1) * n
            base = (core * 4 + 3) * n
            for operand, start in ((3, 0), (4, half)):
                a, b = max(lo, start), min(hi, start + half)
                if a < b:
                    pieces.append((core * 5 + operand, a - start, kind, base + a - lo, b - a))
    pieces.sort(key=lambda p: (p[2] == 2, p[3]))
    return pieces


def expert_body(nb, pieces, src_ref, meta_ref, *refs):
    blocks, weights, outs = refs[:nb], refs[nb : nb + 10], refs[nb + 10 : 2 * nb + 10]
    w_ref, t_ref, x_ref, h_ref, p_ref, s_ref, k_ref, t_sem, w_sem, o_sem = refs[2 * nb + 10 :]
    hidden = w_ref.shape[1]
    width = w_ref.shape[2]

    def block_copy(b):
        return pltpu.make_async_copy(blocks[b], t_ref.at[b], t_sem.at[b])

    def piece_copy(i):
        operand, row, kind, to, count = pieces[i]
        return pltpu.make_async_copy(
            weights[operand].at[pl.ds(row, count)],
            w_ref.at[kind, pl.ds(to, count)],
            w_sem.at[i],
        )

    for b in range(nb):
        block_copy(b).start()
    for i in range(len(pieces)):
        piece_copy(i).start()

    slots = lax.broadcasted_iota(jnp.int32, (CAP, 128), 0).astype(jnp.float32) + 1.0
    for b in range(nb):
        place = meta_ref[src_ref[b], 0:1, :]
        weight = meta_ref[src_ref[b], 1:2, :]
        hit = jnp.where(slots == place, 1.0, 0.0)
        k_ref[pl.ds(b * CAP, CAP), :] = jnp.broadcast_to(
            jnp.sum(hit * weight, axis=1, keepdims=True), (CAP, 128)
        )
        s_ref[b] = hit.T.astype(jnp.bfloat16)
        block_copy(b).wait()
        x_ref[pl.ds(b * CAP, CAP), :] = jnp.dot(
            hit.astype(jnp.bfloat16), t_ref[b], preferred_element_type=jnp.float32
        ).astype(jnp.bfloat16)

    waited = 0
    nt = (((1,), (1,)), ((), ()))
    for n in range(0, hidden, NTILE):
        while waited < len(pieces) and pieces[waited][2] < 2 and pieces[waited][3] < n + NTILE:
            piece_copy(waited).wait()
            waited += 1
        rows = pl.ds(n, NTILE)
        gate = lax.dot_general(x_ref[...], w_ref[0, rows, :], nt, preferred_element_type=jnp.float32)
        up = lax.dot_general(x_ref[...], w_ref[1, rows, :], nt, preferred_element_type=jnp.float32)
        h_ref[:, rows] = (gate / (1.0 + jnp.exp(-gate)) * up).astype(jnp.bfloat16)
    while waited < len(pieces):
        piece_copy(waited).wait()
        waited += 1

    @pl.loop(0, width // CTILE)
    def _(c):
        cols = pl.ds(pl.multiple_of(c * CTILE, CTILE), CTILE)
        out = jnp.dot(h_ref[...], w_ref[2, :, cols], preferred_element_type=jnp.float32)
        out = (out * jnp.tile(k_ref[...], (1, CTILE // 128))).astype(jnp.bfloat16)
        for b in range(nb):
            p_ref[b, :, cols] = jnp.dot(
                s_ref[b], out[b * CAP : (b + 1) * CAP], preferred_element_type=jnp.float32
            ).astype(jnp.bfloat16)

    for b in range(nb):
        pltpu.make_async_copy(p_ref.at[b], outs[b], o_sem.at[b]).start()
    for b in range(nb):
        pltpu.make_async_copy(p_ref.at[b], outs[b], o_sem.at[b]).wait()


def expert_blocks(src, meta, blocks, weights):
    nb = len(blocks)
    rows, width = blocks[0].shape
    n = weights[0].shape[0] // 3
    hidden = 8 * n
    pieces = weight_pieces(n)
    m = nb * CAP
    anywhere = pl.BlockSpec(memory_space=pl.ANY)
    flops = 2 * m * width * hidden * 3 + 4 * m * rows * width
    moved = 2 * (3 * hidden * width + 2 * nb * rows * width)
    return pl.pallas_call(
        functools.partial(expert_body, nb, pieces),
        out_shape=[jax.ShapeDtypeStruct((rows, width), jnp.bfloat16)] * nb,
        in_specs=[
            pl.BlockSpec(memory_space=pltpu.SMEM),
            pl.BlockSpec(memory_space=pltpu.VMEM),
        ]
        + [anywhere] * (nb + 10),
        out_specs=[anywhere] * nb,
        scratch_shapes=[
            pltpu.VMEM((3, hidden, width), jnp.bfloat16),
            pltpu.VMEM((nb, rows, width), jnp.bfloat16),
            pltpu.VMEM((m, width), jnp.bfloat16),
            pltpu.VMEM((m, hidden), jnp.bfloat16),
            pltpu.VMEM((nb, rows, width), jnp.bfloat16),
            pltpu.VMEM((nb, rows, CAP), jnp.bfloat16),
            pltpu.VMEM((m, 128), jnp.float32),
            pltpu.SemaphoreType.DMA((nb,)),
            pltpu.SemaphoreType.DMA((len(pieces),)),
            pltpu.SemaphoreType.DMA((nb,)),
        ],
        compiler_params=pltpu.CompilerParams(vmem_limit_bytes=50 << 20),
        cost_estimate=pl.CostEstimate(flops=flops, bytes_accessed=moved, transcendentals=m * hidden),
        name="expert_blocks_%d" % nb,
    )(src, meta, *blocks, *weights)


def per_device(tokens, expert_ids, gate_fixed, w_gate, w_up, w_down):
    me = lax.axis_index("exp")
    blocks = gather_tokens(tokens)
    weights = gather_weights(jnp.concatenate([w_gate[0].T, w_up[0].T, w_down[0]], axis=0))

    hit = expert_ids.T[None] == jnp.arange(EXPERTS, dtype=jnp.int32)[:, None, None]
    routed = jnp.any(hit, axis=1).astype(jnp.int32)
    place = jnp.cumsum(routed, axis=1) * routed
    gate = jnp.sum(jnp.where(hit, gate_fixed.T[None], 0), axis=1)
    meta = jnp.stack([place.astype(jnp.float32), gate.astype(jnp.float32) / 65536.0], axis=1)
    meta = lax.all_to_all(meta, "exp", split_axis=0, concat_axis=0, tiled=True)

    partial = {}
    for batch in BATCHES:
        dz = jnp.array([o[0] for o in batch], jnp.int32)
        dy = jnp.array([o[1] for o in batch], jnp.int32)
        src = (((me >> 2) + dz) & 3) * 4 + ((me + dy) & 3)
        outs = expert_blocks(src, meta, [blocks[o] for o in batch], weights)
        partial.update(zip(batch, outs))
    return reduce_back(partial)


def solution(mesh):
    in_specs = (
        P(("grp", "exp"), None),
        P(("grp", "exp"), None),
        P(("grp", "exp"), None),
        P("exp", None, "grp"),
        P("exp", None, "grp"),
        P("exp", "grp", None),
    )
    out_specs = P(("grp", "exp"), None)
    return jax.shard_map(
        per_device, mesh=mesh, in_specs=in_specs, out_specs=out_specs, check_vma=False
    )
```

```python
import functools

import jax
import jax.numpy as jnp
from jax import lax
from jax.experimental import pallas as pl
from jax.experimental.pallas import tpu as pltpu
from jax.sharding import PartitionSpec as P


EXPERTS = 16
CAP = 80
NTILE = 256
CTILE = 512


TREE = {
    (1, 0): ((1, 0), (0, 0)),
    (-1, 0): ((-1, 0), (0, 0)),
    (0, 1): ((0, 1), (0, 0)),
    (0, -1): ((0, -1), (0, 0)),
    (-1, -1): ((-1, 0), (0, -1)),
    (1, -1): ((0, -1), (1, 0)),
    (-1, 1): ((0, 1), (-1, 0)),
    (1, 1): ((1, 0), (0, 1)),
    (2, -1): ((-1, 0), (-1, -1)),
    (-1, 2): ((0, -1), (-1, -1)),
    (0, 2): ((0, 1), (0, 1)),
    (2, 0): ((1, 0), (1, 0)),
    (2, 2): ((0, -1), (2, -1)),
    (1, 2): ((0, 1), (1, 1)),
    (2, 1): ((1, 0), (1, 1)),
}

BATCHES = [
    [(2, 2), (2, 1), (1, 2)],
    [(2, -1), (-1, 2), (2, 0), (0, 2)],
    [(-1, -1), (1, 1), (1, -1), (-1, 1)],
    [(0, 0), (1, 0), (-1, 0), (0, 1), (0, -1)],
]


def get_exp(x, dz, dy):
    pairs = [
        (((z + dz) % 4) * 4 + (y + dy) % 4, z * 4 + y) for z in range(4) for y in range(4)
    ]
    return lax.ppermute(x, "exp", pairs)


def get_x(v, dx):
    pairs = [(((x + dx) % 4) * 2 + c, x * 2 + c) for x in range(4) for c in range(2)]
    return lax.ppermute(v, "grp", pairs)


def get_core(v):
    pairs = [(x * 2 + 1 - c, x * 2 + c) for x in range(4) for c in range(2)]
    return lax.ppermute(v, "grp", pairs)


def gather_weights(w):
    half = w.shape[0] // 2
    right = get_x(w, 1)
    left = get_x(w, -1)
    far_a = get_x(right[:half], 1)
    far_b = get_x(left[half:], -1)
    mine = [w, right, left, far_a, far_b]
    other = []
    for v in mine:
        other.append(get_core(v))
    return mine + other


def gather_tokens(t):
    blocks = {(0, 0): t}
    for offset, (way, before) in TREE.items():
        blocks[offset] = get_exp(blocks[before], *way)
    return blocks


def reduce_back(partial):
    terms = {offset: [value] for offset, value in partial.items()}
    for offset, (way, before) in reversed(TREE.items()):
        own = terms[offset]
        value = own[0]
        if len(own) > 1:
            value = sum(v.astype(jnp.float32) for v in own).astype(jnp.bfloat16)
        terms[before].append(get_exp(value, -way[0], -way[1]))
    return sum(v.astype(jnp.float32) for v in terms[0, 0]).astype(jnp.bfloat16)


def weight_pieces(n):
    half = 3 * n // 2
    pieces = []

    def cut(operand, row, kind, to, count):
        while count:
            part = min(count, NTILE - to % NTILE)
            pieces.append((operand, row, kind, to, part))
            row, to, count = row + part, to + part, count - part

    for core in range(2):
        for k in range(3):
            for kind in range(3):
                cut(core * 5 + k, kind * n, kind, (core * 4 + k) * n, n)
        for kind in range(3):
            lo, hi = kind * n, (kind + 1) * n
            base = (core * 4 + 3) * n
            for operand, start in ((3, 0), (4, half)):
                a, b = max(lo, start), min(hi, start + half)
                if a < b:
                    cut(core * 5 + operand, a - start, kind, base + a - lo, b - a)
    pieces.sort(key=lambda p: (p[2] == 2, p[3]))
    return pieces


def expert_body(nb, pieces, src_ref, meta_ref, *refs):
    blocks, weights, outs = refs[:nb], refs[nb : nb + 10], refs[nb + 10 : 2 * nb + 10]
    w_ref, t_ref, x_ref, h_ref, o_ref, p_ref, s_ref, k_ref, t_sem, w_sem, o_sem = refs[2 * nb + 10 :]
    hidden = w_ref.shape[1]
    width = w_ref.shape[2]
    tiles = hidden // NTILE

    for b in range(nb):
        pltpu.make_async_copy(blocks[b], t_ref.at[b], t_sem.at[b]).start()
    for operand, row, kind, to, count in pieces:
        pltpu.make_async_copy(
            weights[operand].at[pl.ds(row, count)],
            w_ref.at[kind, pl.ds(to, count)],
            w_sem.at[tiles if kind == 2 else to // NTILE],
        ).start()

    slots = lax.broadcasted_iota(jnp.int32, (CAP, 128), 0).astype(jnp.float32) + 1.0

    @pl.loop(0, nb)
    def _(b):
        source = src_ref[b]
        hit = jnp.where(slots == meta_ref[source, 0:1, :], 1.0, 0.0)
        scale = jnp.sum(hit * meta_ref[source, 1:2, :], axis=1, keepdims=True)
        rows = pl.ds(pl.multiple_of(b * CAP, CAP), CAP)
        k_ref[rows, :] = jnp.broadcast_to(scale, (CAP, 128))
        s_ref[b] = hit.T.astype(jnp.bfloat16)
        pltpu.make_async_copy(t_ref.at[b], t_ref.at[b], t_sem.at[b]).wait()
        x_ref[rows, :] = jnp.dot(
            hit.astype(jnp.bfloat16), t_ref[b], preferred_element_type=jnp.float32
        ).astype(jnp.bfloat16)

    nt = (((1,), (1,)), ((), ()))

    @pl.loop(0, tiles)
    def _(n):
        rows = pl.ds(pl.multiple_of(n * NTILE, NTILE), NTILE)
        both = w_ref.at[pl.ds(0, 2), rows]
        pltpu.make_async_copy(both, both, w_sem.at[n]).wait()
        gate = lax.dot_general(x_ref[...], w_ref[0, rows, :], nt, preferred_element_type=jnp.float32)
        up = lax.dot_general(x_ref[...], w_ref[1, rows, :], nt, preferred_element_type=jnp.float32)
        h_ref[:, rows] = (gate / (1.0 + jnp.exp(-gate)) * up).astype(jnp.bfloat16)

    pltpu.make_async_copy(w_ref.at[2], w_ref.at[2], w_sem.at[tiles]).wait()

    @pl.loop(0, width // CTILE)
    def _(c):
        cols = pl.ds(pl.multiple_of(c * CTILE, CTILE), CTILE)
        out = jnp.dot(h_ref[...], w_ref[2, :, cols], preferred_element_type=jnp.float32)
        o_ref[...] = (out * jnp.tile(k_ref[...], (1, CTILE // 128))).astype(jnp.bfloat16)

        @pl.loop(0, nb)
        def _(b):
            rows = pl.ds(pl.multiple_of(b * CAP, CAP), CAP)
            p_ref[b, :, cols] = jnp.dot(
                s_ref[b], o_ref[rows, :], preferred_element_type=jnp.float32
            ).astype(jnp.bfloat16)

    for b in range(nb):
        pltpu.make_async_copy(p_ref.at[b], outs[b], o_sem.at[b]).start()
    for b in range(nb):
        pltpu.make_async_copy(p_ref.at[b], outs[b], o_sem.at[b]).wait()


def expert_blocks(src, meta, blocks, weights):
    nb = len(blocks)
    rows, width = blocks[0].shape
    n = weights[0].shape[0] // 3
    hidden = 8 * n
    pieces = weight_pieces(n)
    m = nb * CAP
    anywhere = pl.BlockSpec(memory_space=pl.ANY)
    flops = 2 * m * width * hidden * 3 + 4 * m * rows * width
    moved = 2 * (3 * hidden * width + 2 * nb * rows * width)
    return pl.pallas_call(
        functools.partial(expert_body, nb, pieces),
        out_shape=[jax.ShapeDtypeStruct((rows, width), jnp.bfloat16)] * nb,
        in_specs=[
            pl.BlockSpec(memory_space=pltpu.SMEM),
            pl.BlockSpec(memory_space=pltpu.VMEM),
        ]
        + [anywhere] * (nb + 10),
        out_specs=[anywhere] * nb,
        scratch_shapes=[
            pltpu.VMEM((3, hidden, width), jnp.bfloat16),
            pltpu.VMEM((nb, rows, width), jnp.bfloat16),
            pltpu.VMEM((m, width), jnp.bfloat16),
            pltpu.VMEM((m, hidden), jnp.bfloat16),
            pltpu.VMEM((m, CTILE), jnp.bfloat16),
            pltpu.VMEM((nb, rows, width), jnp.bfloat16),
            pltpu.VMEM((nb, rows, CAP), jnp.bfloat16),
            pltpu.VMEM((m, 128), jnp.float32),
            pltpu.SemaphoreType.DMA((nb,)),
            pltpu.SemaphoreType.DMA((hidden // NTILE + 1,)),
            pltpu.SemaphoreType.DMA((nb,)),
        ],
        compiler_params=pltpu.CompilerParams(vmem_limit_bytes=50 << 20),
        cost_estimate=pl.CostEstimate(flops=flops, bytes_accessed=moved, transcendentals=m * hidden),
    )(src, meta, *blocks, *weights)


def per_device(tokens, expert_ids, gate_fixed, w_gate, w_up, w_down):
    me = lax.axis_index("exp")
    blocks = gather_tokens(tokens)
    weights = gather_weights(jnp.concatenate([w_gate[0].T, w_up[0].T, w_down[0]], axis=0))

    hit = expert_ids.T[None] == jnp.arange(EXPERTS, dtype=jnp.int32)[:, None, None]
    routed = jnp.any(hit, axis=1).astype(jnp.int32)
    place = jnp.cumsum(routed, axis=1) * routed
    gate = jnp.sum(jnp.where(hit, gate_fixed.T[None], 0), axis=1)
    meta = jnp.stack([place.astype(jnp.float32), gate.astype(jnp.float32) / 65536.0], axis=1)
    meta = lax.all_to_all(meta, "exp", split_axis=0, concat_axis=0, tiled=True)

    partial = {}
    for batch in BATCHES:
        dz = jnp.array([o[0] for o in batch], jnp.int32)
        dy = jnp.array([o[1] for o in batch], jnp.int32)
        src = (((me >> 2) + dz) & 3) * 4 + ((me + dy) & 3)
        outs = expert_blocks(src, meta, [blocks[o] for o in batch], weights)
        partial.update(zip(batch, outs))
    return reduce_back(partial)


def solution(mesh):
    in_specs = (
        P(("grp", "exp"), None),
        P(("grp", "exp"), None),
        P(("grp", "exp"), None),
        P("exp", None, "grp"),
        P("exp", None, "grp"),
        P("exp", "grp", None),
    )
    out_specs = P(("grp", "exp"), None)

    return jax.shard_map(
        per_device, mesh=mesh, in_specs=in_specs, out_specs=out_specs, check_vma=False
    )
```

```python
import functools

import jax
import jax.numpy as jnp
from jax import lax
from jax.experimental import pallas as pl
from jax.experimental.pallas import tpu as pltpu
from jax.sharding import PartitionSpec as P


EXPERTS = 16
CAP = 80
NTILE = 256
CTILE = 512


TREE = {
    (1, 0): [(0, 128, (1, 0), (0, 0))],
    (-1, 0): [(0, 128, (-1, 0), (0, 0))],
    (0, 1): [(0, 128, (0, 1), (0, 0))],
    (0, -1): [(0, 128, (0, -1), (0, 0))],
    (-1, -1): [(0, 128, (-1, 0), (0, -1))],
    (1, -1): [(0, 128, (0, -1), (1, 0))],
    (-1, 1): [(0, 128, (0, 1), (-1, 0))],
    (1, 1): [(0, 128, (1, 0), (0, 1))],
    (2, -1): [(0, 128, (-1, 0), (-1, -1))],
    (-1, 2): [(0, 128, (0, -1), (-1, -1))],
    (0, 2): [(0, 128, (0, 1), (0, 1))],
    (2, 0): [(0, 128, (1, 0), (1, 0))],
    (2, 2): [(0, 64, (0, -1), (2, -1)), (64, 64, (-1, 0), (-1, 2))],
    (1, 2): [(0, 128, (0, 1), (1, 1))],
    (2, 1): [(0, 128, (1, 0), (1, 1))],
}

BATCHES = [
    [(2, 2), (2, 1), (1, 2)],
    [(2, -1), (-1, 2), (2, 0), (0, 2)],
    [(-1, -1), (1, 1), (1, -1), (-1, 1)],
    [(0, 0), (1, 0), (-1, 0), (0, 1), (0, -1)],
]


def get_exp(x, dz, dy):
    pairs = [
        (((z + dz) % 4) * 4 + (y + dy) % 4, z * 4 + y) for z in range(4) for y in range(4)
    ]
    return lax.ppermute(x, "exp", pairs)


def get_x(v, dx):
    pairs = [(((x + dx) % 4) * 2 + c, x * 2 + c) for x in range(4) for c in range(2)]
    return lax.ppermute(v, "grp", pairs)


def get_core(v):
    pairs = [(x * 2 + 1 - c, x * 2 + c) for x in range(4) for c in range(2)]
    return lax.ppermute(v, "grp", pairs)


def gather_weights(w):
    half = w.shape[0] // 2
    right = get_x(w, 1)
    left = get_x(w, -1)
    far_a = get_x(right[:half], 1)
    far_b = get_x(left[half:], -1)
    mine = [w, right, left, far_a, far_b]
    other = []
    for v in mine:
        other.append(get_core(v))
    return mine + other


def gather_tokens(t):
    blocks = {(0, 0): [t]}
    for offset, parts in TREE.items():
        blocks[offset] = []
        for row, rows, way, before in parts:
            (source,) = blocks[before]
            if rows < source.shape[0]:
                source = source[row : row + rows]
            blocks[offset].append(get_exp(source, *way))
    return blocks


def add_up(value, extra):
    rows = value.shape[0]
    cuts = sorted({0, rows} | {r for r, _ in extra} | {r + v.shape[0] for r, v in extra})
    pieces = []
    for lo, hi in zip(cuts, cuts[1:]):
        total = value[lo:hi].astype(jnp.float32)
        for row, v in extra:
            if row <= lo and hi <= row + v.shape[0]:
                total = total + v[lo - row : hi - row].astype(jnp.float32)
        pieces.append(total.astype(jnp.bfloat16))
    return pieces[0] if len(pieces) == 1 else jnp.concatenate(pieces, axis=0)


def reduce_back(partial):
    extra = {offset: [] for offset in partial}
    for offset, parts in reversed(TREE.items()):
        values = partial[offset]
        if extra[offset]:
            values = [add_up(values[0], extra[offset])]
        for i, (row, rows, way, before) in enumerate(parts):
            extra[before].append((row, get_exp(values[i], -way[0], -way[1])))
    return add_up(partial[0, 0][0], extra[0, 0])


def weight_pieces(n):
    half = 3 * n // 2
    pieces = []

    def cut(operand, row, kind, to, count):
        while count:
            part = min(count, NTILE - to % NTILE)
            pieces.append((operand, row, kind, to, part))
            row, to, count = row + part, to + part, count - part

    for core in range(2):
        for k in range(3):
            for kind in range(3):
                cut(core * 5 + k, kind * n, kind, (core * 4 + k) * n, n)
        for kind in range(3):
            lo, hi = kind * n, (kind + 1) * n
            base = (core * 4 + 3) * n
            for operand, start in ((3, 0), (4, half)):
                a, b = max(lo, start), min(hi, start + half)
                if a < b:
                    cut(core * 5 + operand, a - start, kind, base + a - lo, b - a)
    pieces.sort(key=lambda p: (p[2] == 2, p[3]))
    return pieces


def expert_body(nb, parts, pieces, src_ref, meta_ref, *refs):
    np_ = len(parts)
    inputs, weights, outs = refs[:np_], refs[np_ : np_ + 10], refs[np_ + 10 : 2 * np_ + 10]
    w_ref, t_ref, x_ref, h_ref, o_ref, p_ref, s_ref, k_ref, t_sem, w_sem, o_sem = refs[2 * np_ + 10 :]
    hidden = w_ref.shape[1]
    width = w_ref.shape[2]
    tiles = hidden // NTILE

    for i, (b, row, rows) in enumerate(parts):
        pltpu.make_async_copy(inputs[i], t_ref.at[b, pl.ds(row, rows)], t_sem.at[b]).start()

    def fetch(stage):
        for operand, row, kind, to, count in pieces:
            if (tiles if kind == 2 else to // NTILE) == stage:
                pltpu.make_async_copy(
                    weights[operand].at[pl.ds(row, count)],
                    w_ref.at[kind, pl.ds(to, count)],
                    w_sem.at[stage],
                ).start()

    fetch(0)

    def out_copy(i):
        b, row, rows = parts[i]
        return pltpu.make_async_copy(p_ref.at[b, pl.ds(row, rows)], outs[i], o_sem.at[i])

    slots = lax.broadcasted_iota(jnp.int32, (CAP, 128), 0).astype(jnp.float32) + 1.0

    @pl.loop(0, nb)
    def _(b):
        source = src_ref[b]
        hit = jnp.where(slots == meta_ref[source, 0:1, :], 1.0, 0.0)
        scale = jnp.sum(hit * meta_ref[source, 1:2, :], axis=1, keepdims=True)
        rows = pl.ds(pl.multiple_of(b * CAP, CAP), CAP)
        k_ref[rows, :] = jnp.broadcast_to(scale, (CAP, 128))
        s_ref[b] = hit.T.astype(jnp.bfloat16)
        pltpu.make_async_copy(t_ref.at[b], t_ref.at[b], t_sem.at[b]).wait()
        x_ref[rows, :] = jnp.dot(
            hit.astype(jnp.bfloat16), t_ref[b], preferred_element_type=jnp.float32
        ).astype(jnp.bfloat16)

    fetch(1)

    nt = (((1,), (1,)), ((), ()))

    @pl.loop(0, tiles)
    def _(n):
        rows = pl.ds(pl.multiple_of(n * NTILE, NTILE), NTILE)
        both = w_ref.at[pl.ds(0, 2), rows]
        pltpu.make_async_copy(both, both, w_sem.at[n]).wait()
        for stage in range(2, tiles + 1):

            @pl.when(n == stage - 2)
            def _():
                fetch(stage)

        gate = lax.dot_general(x_ref[...], w_ref[0, rows, :], nt, preferred_element_type=jnp.float32)
        up = lax.dot_general(x_ref[...], w_ref[1, rows, :], nt, preferred_element_type=jnp.float32)
        h_ref[:, rows] = (gate / (1.0 + jnp.exp(-gate)) * up).astype(jnp.bfloat16)

    pltpu.make_async_copy(w_ref.at[2], w_ref.at[2], w_sem.at[tiles]).wait()

    @pl.loop(0, width // CTILE)
    def _(c):
        cols = pl.ds(pl.multiple_of(c * CTILE, CTILE), CTILE)
        out = jnp.dot(h_ref[...], w_ref[2, :, cols], preferred_element_type=jnp.float32)
        o_ref[:, cols] = (out * jnp.tile(k_ref[...], (1, CTILE // 128))).astype(jnp.bfloat16)

    for b in range(nb):
        p_ref[b] = jnp.dot(
            s_ref[b], o_ref[b * CAP : (b + 1) * CAP, :], preferred_element_type=jnp.float32
        ).astype(jnp.bfloat16)
        for i, (block, row, rows) in enumerate(parts):
            if block == b:
                out_copy(i).start()
    for i in range(np_):
        out_copy(i).wait()


def expert_blocks(src, meta, blocks, weights):
    nb = len(blocks)
    parts, inputs = [], []
    for b, block in enumerate(blocks):
        row = 0
        for part in block:
            parts.append((b, row, part.shape[0]))
            inputs.append(part)
            row += part.shape[0]
    rows, width = row, inputs[0].shape[1]
    n = weights[0].shape[0] // 3
    hidden = 8 * n
    pieces = weight_pieces(n)
    m = nb * CAP
    anywhere = pl.BlockSpec(memory_space=pl.ANY)
    flops = 2 * m * width * hidden * 3 + 4 * m * rows * width
    moved = 2 * (3 * hidden * width + 2 * nb * rows * width)
    outs = pl.pallas_call(
        functools.partial(expert_body, nb, parts, pieces),
        out_shape=[jax.ShapeDtypeStruct(v.shape, jnp.bfloat16) for v in inputs],
        in_specs=[
            pl.BlockSpec(memory_space=pltpu.SMEM),
            pl.BlockSpec(memory_space=pltpu.VMEM),
        ]
        + [anywhere] * (len(parts) + 10),
        out_specs=[anywhere] * len(parts),
        scratch_shapes=[
            pltpu.VMEM((3, hidden, width), jnp.bfloat16),
            pltpu.VMEM((nb, rows, width), jnp.bfloat16),
            pltpu.VMEM((m, width), jnp.bfloat16),
            pltpu.VMEM((m, hidden), jnp.bfloat16),
            pltpu.VMEM((m, width), jnp.bfloat16),
            pltpu.VMEM((nb, rows, width), jnp.bfloat16),
            pltpu.VMEM((nb, rows, CAP), jnp.bfloat16),
            pltpu.VMEM((m, 128), jnp.float32),
            pltpu.SemaphoreType.DMA((nb,)),
            pltpu.SemaphoreType.DMA((hidden // NTILE + 1,)),
            pltpu.SemaphoreType.DMA((len(parts),)),
        ],
        compiler_params=pltpu.CompilerParams(vmem_limit_bytes=50 << 20),
        cost_estimate=pl.CostEstimate(flops=flops, bytes_accessed=moved, transcendentals=m * hidden),
    )(src, meta, *inputs, *weights)
    return [[v for v, part in zip(outs, parts) if part[0] == b] for b in range(nb)]


def per_device(tokens, expert_ids, gate_fixed, w_gate, w_up, w_down):
    me = lax.axis_index("exp")
    blocks = gather_tokens(tokens)
    weights = gather_weights(jnp.concatenate([w_gate[0].T, w_up[0].T, w_down[0]], axis=0))

    hit = expert_ids.T[None] == jnp.arange(EXPERTS, dtype=jnp.int32)[:, None, None]
    routed = jnp.any(hit, axis=1).astype(jnp.int32)
    place = jnp.cumsum(routed, axis=1) * routed
    gate = jnp.sum(jnp.where(hit, gate_fixed.T[None], 0), axis=1)
    meta = jnp.stack([place.astype(jnp.float32), gate.astype(jnp.float32) / 65536.0], axis=1)
    meta = lax.all_to_all(meta, "exp", split_axis=0, concat_axis=0, tiled=True)

    partial = {}
    for batch in BATCHES:
        dz = jnp.array([o[0] for o in batch], jnp.int32)
        dy = jnp.array([o[1] for o in batch], jnp.int32)
        src = (((me >> 2) + dz) & 3) * 4 + ((me + dy) & 3)
        outs = expert_blocks(src, meta, [blocks[o] for o in batch], weights)
        partial.update(zip(batch, outs))
    return reduce_back(partial)


def solution(mesh):
    in_specs = (
        P(("grp", "exp"), None),
        P(("grp", "exp"), None),
        P(("grp", "exp"), None),
        P("exp", None, "grp"),
        P("exp", None, "grp"),
        P("exp", "grp", None),
    )
    out_specs = P(("grp", "exp"), None)

    return jax.shard_map(
        per_device, mesh=mesh, in_specs=in_specs, out_specs=out_specs, check_vma=False
    )
```

```python
import functools

import jax
import jax.numpy as jnp
from jax import lax
from jax.experimental import pallas as pl
from jax.experimental.pallas import tpu as pltpu
from jax.sharding import PartitionSpec as P


EXPERTS = 16
CAP = 80
NTILE = 256
CTILE = 512


TREE = {
    (1, 0): [(0, 128, (1, 0), (0, 0))],
    (-1, 0): [(0, 128, (-1, 0), (0, 0))],
    (0, 1): [(0, 128, (0, 1), (0, 0))],
    (0, -1): [(0, 128, (0, -1), (0, 0))],
    (-1, -1): [(0, 64, (-1, 0), (0, -1)), (64, 64, (-1, 0), (0, -1))],
    (1, -1): [(0, 128, (0, -1), (1, 0))],
    (-1, 1): [(0, 128, (0, 1), (-1, 0))],
    (1, 1): [(0, 128, (1, 0), (0, 1))],
    (2, -1): [(0, 64, (-1, 0), (-1, -1)), (64, 64, (-1, 0), (-1, -1))],
    (-1, 2): [(0, 64, (0, -1), (-1, -1)), (64, 64, (0, -1), (-1, -1))],
    (0, 2): [(0, 128, (0, 1), (0, 1))],
    (2, 0): [(0, 128, (1, 0), (1, 0))],
    (2, 2): [(0, 64, (0, -1), (2, -1)), (64, 64, (-1, 0), (-1, 2))],
    (1, 2): [(0, 128, (0, 1), (1, 1))],
    (2, 1): [(0, 128, (1, 0), (1, 1))],
}

WHOLE = {o: [(0, 128) + parts[0][2:]] for o, parts in TREE.items()}
BACK = {
    **WHOLE,
    (2, 2): TREE[2, 2],
    (2, 0): [(0, 96, (1, 0), (1, 0)), (96, 32, (-1, 0), (-1, 0))],
    (0, 2): [(0, 96, (0, 1), (0, 1)), (96, 32, (0, -1), (0, -1))],
}

BATCHES = [
    [(2, 2), (2, 1), (1, 2)],
    [(2, -1), (-1, 2), (2, 0), (0, 2)],
    [(-1, -1), (1, 1), (1, -1), (-1, 1)],
    [(1, 0), (-1, 0), (0, 1), (0, -1)],
    [(0, 0)],
]


def get_exp(x, dz, dy):
    pairs = [
        (((z + dz) % 4) * 4 + (y + dy) % 4, z * 4 + y) for z in range(4) for y in range(4)
    ]
    return lax.ppermute(x, "exp", pairs)


def get_x(v, dx):
    pairs = [(((x + dx) % 4) * 2 + c, x * 2 + c) for x in range(4) for c in range(2)]
    return lax.ppermute(v, "grp", pairs)


def get_core(v):
    pairs = [(x * 2 + 1 - c, x * 2 + c) for x in range(4) for c in range(2)]
    return lax.ppermute(v, "grp", pairs)


def gather_weights(gate, up, down):
    mid = gate.shape[0] // 2
    own = [
        jnp.concatenate([gate, up[:mid]], axis=0),
        jnp.concatenate([up[mid:], down], axis=0),
    ]
    right, left = [None, None], [None, None]
    for i in (0, 1):
        right[i] = get_x(own[i], 1)
        left[i] = get_x(own[i], -1)
    far = []
    for i, near in enumerate((right[0], left[1])):
        far.append(get_x(near, 1 - 2 * i))
    mine = own + right + left + far
    other = []
    for v in mine:
        other.append(get_core(v))
    return mine + other


def take(parts, row, rows):
    at = 0
    for part in parts:
        size = part.shape[0]
        if at <= row and row + rows <= at + size:
            return part if size == rows else part[row - at : row - at + rows]
        at += size
    raise ValueError("part")


def gather_tokens(t):
    blocks = {(0, 0): [t]}
    for offset, parts in TREE.items():
        blocks[offset] = []
        for row, rows, way, before in parts:
            source = take(blocks[before], row, rows)
            blocks[offset].append(get_exp(source, *way))
    return blocks


def add_up(value, extra):
    rows = value.shape[0]
    total = value.astype(jnp.float32)
    for row, v in extra:
        below = rows - row - v.shape[0]
        if row or below:
            v = jnp.pad(v, ((row, below), (0, 0)))
        total = total + v.astype(jnp.float32)
    return total.astype(jnp.bfloat16)


def reduce_back(partial):
    extra = {offset: [] for offset in partial}
    for offset, parts in reversed(BACK.items()):
        values = partial[offset]
        if extra[offset]:
            values = [add_up(values[0], extra[offset])]
        for i, (row, rows, way, before) in enumerate(parts):
            extra[before].append((row, get_exp(values[i], -way[0], -way[1])))
    return add_up(partial[0, 0][0], extra[0, 0])


def weight_pieces(n):
    half = 3 * n // 2
    pieces = []

    def cut(operand, row, kind, to, count):
        while count:
            part = min(count, NTILE - to % NTILE)
            pieces.append((operand, row, kind, to, part))
            row, to, count = row + part, to + part, count - part

    for shard in range(8):
        for kind in range(3):
            lo, hi = kind * n, (kind + 1) * n
            for part in range(2):
                start = part * half
                a, b = max(lo, start), min(hi, start + half)
                if a < b:
                    cut(2 * shard + part, a - start, kind, shard * n + a - lo, b - a)
    pieces.sort(key=lambda p: (p[2] == 2, p[3]))
    return pieces


def expert_body(nb, parts, out_parts, pieces, src_ref, meta_ref, *refs):
    weights, refs = refs[:16], refs[16:]
    inputs, refs = refs[: len(parts)], refs[len(parts) :]
    outs, refs = refs[: len(out_parts)], refs[len(out_parts) :]
    w_ref, t_ref, x_ref, h_ref, o_ref, p_ref, s_ref, k_ref, t_sem, w_sem, o_sem = refs
    hidden = w_ref.shape[1]
    width = w_ref.shape[2]
    tiles = hidden // NTILE

    for i, (b, row, rows) in enumerate(parts):
        pltpu.make_async_copy(inputs[i], t_ref.at[b, pl.ds(row, rows)], t_sem.at[b]).start()

    def fetch(stage):
        for operand, row, kind, to, count in pieces:
            if (tiles if kind == 2 else to // NTILE) == stage:
                pltpu.make_async_copy(
                    weights[operand].at[pl.ds(row, count)],
                    w_ref.at[kind, pl.ds(to, count)],
                    w_sem.at[stage],
                ).start()

    fetch(0)

    def out_copy(i):
        b, row, rows = out_parts[i]
        return pltpu.make_async_copy(p_ref.at[b, pl.ds(row, rows)], outs[i], o_sem.at[i])

    slots = lax.broadcasted_iota(jnp.int32, (CAP, 128), 0).astype(jnp.float32) + 1.0

    @pl.loop(0, nb)
    def _(b):
        source = src_ref[b]
        hit = jnp.where(slots == meta_ref[source, 0:1, :], 1.0, 0.0)
        scale = jnp.sum(hit * meta_ref[source, 1:2, :], axis=1, keepdims=True)
        rows = pl.ds(pl.multiple_of(b * CAP, CAP), CAP)
        k_ref[rows, :] = jnp.broadcast_to(scale, (CAP, 128))
        s_ref[b] = hit.T.astype(jnp.bfloat16)
        pltpu.make_async_copy(t_ref.at[b], t_ref.at[b], t_sem.at[b]).wait()
        x_ref[rows, :] = jnp.dot(
            hit.astype(jnp.bfloat16), t_ref[b], preferred_element_type=jnp.float32
        ).astype(jnp.bfloat16)

    fetch(1)

    nt = (((1,), (1,)), ((), ()))

    @pl.loop(0, tiles)
    def _(n):
        rows = pl.ds(pl.multiple_of(n * NTILE, NTILE), NTILE)
        both = w_ref.at[pl.ds(0, 2), rows]
        pltpu.make_async_copy(both, both, w_sem.at[n]).wait()
        for stage in range(2, tiles + 1):

            @pl.when(n == stage - 2)
            def _():
                fetch(stage)

        gate = lax.dot_general(x_ref[...], w_ref[0, rows, :], nt, preferred_element_type=jnp.float32)
        up = lax.dot_general(x_ref[...], w_ref[1, rows, :], nt, preferred_element_type=jnp.float32)
        h_ref[:, rows] = (gate / (1.0 + jnp.exp(-gate)) * up).astype(jnp.bfloat16)

    pltpu.make_async_copy(w_ref.at[2], w_ref.at[2], w_sem.at[tiles]).wait()

    @pl.loop(0, width // CTILE)
    def _(c):
        cols = pl.ds(pl.multiple_of(c * CTILE, CTILE), CTILE)
        out = jnp.dot(h_ref[...], w_ref[2, :, cols], preferred_element_type=jnp.float32)
        o_ref[:, cols] = (out * jnp.tile(k_ref[...], (1, CTILE // 128))).astype(jnp.bfloat16)

    @pl.loop(0, nb)
    def _(b):
        rows = pl.ds(pl.multiple_of(b * CAP, CAP), CAP)
        p_ref[b] = jnp.dot(
            s_ref[b], o_ref[rows, :], preferred_element_type=jnp.float32
        ).astype(jnp.bfloat16)
        for i, part in enumerate(out_parts):

            @pl.when(b == part[0])
            def _():
                out_copy(i).start()

    for i in range(len(out_parts)):
        out_copy(i).wait()


def expert_blocks(src, meta, blocks, weights, cuts):
    nb = len(blocks)
    parts, inputs = [], []
    for b, block in enumerate(blocks):
        row = 0
        for part in block:
            parts.append((b, row, part.shape[0]))
            inputs.append(part)
            row += part.shape[0]
    rows, width = row, inputs[0].shape[1]
    out_parts = [(b, row, size) for b, cut in enumerate(cuts) for row, size in cut]
    n = 2 * weights[0].shape[0] // 3
    hidden = 8 * n
    pieces = weight_pieces(n)
    m = nb * CAP
    anywhere = pl.BlockSpec(memory_space=pl.ANY)
    flops = 2 * m * width * hidden * 3 + 4 * m * rows * width
    moved = 2 * (3 * hidden * width + 2 * nb * rows * width)
    outs = pl.pallas_call(
        functools.partial(expert_body, nb, parts, out_parts, pieces),
        out_shape=[jax.ShapeDtypeStruct((part[2], width), jnp.bfloat16) for part in out_parts],
        in_specs=[
            pl.BlockSpec(memory_space=pltpu.SMEM),
            pl.BlockSpec(memory_space=pltpu.VMEM),
        ]
        + [anywhere] * (16 + len(parts)),
        out_specs=[anywhere] * len(out_parts),
        scratch_shapes=[
            pltpu.VMEM((3, hidden, width), jnp.bfloat16),
            pltpu.VMEM((nb, rows, width), jnp.bfloat16),
            pltpu.VMEM((m, width), jnp.bfloat16),
            pltpu.VMEM((m, hidden), jnp.bfloat16),
            pltpu.VMEM((m, width), jnp.bfloat16),
            pltpu.VMEM((nb, rows, width), jnp.bfloat16),
            pltpu.VMEM((nb, rows, CAP), jnp.bfloat16),
            pltpu.VMEM((m, 128), jnp.float32),
            pltpu.SemaphoreType.DMA((nb,)),
            pltpu.SemaphoreType.DMA((hidden // NTILE + 1,)),
            pltpu.SemaphoreType.DMA((len(out_parts),)),
        ],
        compiler_params=pltpu.CompilerParams(vmem_limit_bytes=50 << 20),
        cost_estimate=pl.CostEstimate(flops=flops, bytes_accessed=moved, transcendentals=m * hidden),
    )(src, meta, *weights, *inputs)
    return [[v for v, part in zip(outs, out_parts) if part[0] == b] for b in range(nb)]


def per_device(tokens, expert_ids, gate_fixed, w_gate, w_up, w_down):
    me = lax.axis_index("exp")
    blocks = gather_tokens(tokens)
    weights = gather_weights(w_gate[0].T, w_up[0].T, w_down[0])

    hit = expert_ids.T[None] == jnp.arange(EXPERTS, dtype=jnp.int32)[:, None, None]
    routed = jnp.any(hit, axis=1).astype(jnp.int32)
    place = jnp.cumsum(routed, axis=1) * routed
    gate = jnp.sum(jnp.where(hit, gate_fixed.T[None], 0), axis=1)
    meta = jnp.stack([place.astype(jnp.float32), gate.astype(jnp.float32) / 65536.0], axis=1)
    meta = lax.all_to_all(meta, "exp", split_axis=0, concat_axis=0, tiled=True)

    partial = {}
    for batch in BATCHES:
        dz = jnp.array([o[0] for o in batch], jnp.int32)
        dy = jnp.array([o[1] for o in batch], jnp.int32)
        src = (((me >> 2) + dz) & 3) * 4 + ((me + dy) & 3)
        cuts = [[part[:2] for part in BACK.get(o, [(0, 128)])] for o in batch]
        outs = expert_blocks(src, meta, [blocks[o] for o in batch], weights, cuts)
        partial.update(zip(batch, outs))
    return reduce_back(partial)


def solution(mesh):
    in_specs = (
        P(("grp", "exp"), None),
        P(("grp", "exp"), None),
        P(("grp", "exp"), None),
        P("exp", None, "grp"),
        P("exp", None, "grp"),
        P("exp", "grp", None),
    )
    out_specs = P(("grp", "exp"), None)

    return jax.shard_map(
        per_device, mesh=mesh, in_specs=in_specs, out_specs=out_specs, check_vma=False
    )
```

```python
import functools

import jax
import jax.numpy as jnp
from jax import lax
from jax.experimental import pallas as pl
from jax.experimental.pallas import tpu as pltpu
from jax.sharding import PartitionSpec as P


EXPERTS = 16
CAP = 80
NTILE = 256
CTILE = 1024


TREE = {
    (1, 0): [(0, 128, (1, 0), (0, 0))],
    (-1, 0): [(0, 128, (-1, 0), (0, 0))],
    (0, 1): [(0, 128, (0, 1), (0, 0))],
    (0, -1): [(0, 128, (0, -1), (0, 0))],
    (-1, -1): [(0, 64, (-1, 0), (0, -1)), (64, 64, (-1, 0), (0, -1))],
    (1, -1): [(0, 128, (0, -1), (1, 0))],
    (-1, 1): [(0, 128, (0, 1), (-1, 0))],
    (1, 1): [(0, 128, (1, 0), (0, 1))],
    (2, -1): [(0, 64, (-1, 0), (-1, -1)), (64, 64, (-1, 0), (-1, -1))],
    (-1, 2): [(0, 64, (0, -1), (-1, -1)), (64, 64, (0, -1), (-1, -1))],
    (0, 2): [(0, 128, (0, 1), (0, 1))],
    (2, 0): [(0, 128, (1, 0), (1, 0))],
    (2, 2): [(0, 64, (0, -1), (2, -1)), (64, 64, (-1, 0), (-1, 2))],
    (1, 2): [(0, 128, (0, 1), (1, 1))],
    (2, 1): [(0, 128, (1, 0), (1, 1))],
}

BACK = {o: [(0, 128) + parts[0][2:]] for o, parts in TREE.items()}
BACK[2, 2] = TREE[2, 2]

BATCHES = [
    [(2, 2), (2, 1), (1, 2)],
    [(2, -1), (-1, 2), (2, 0), (0, 2)],
    [(-1, -1), (1, 1), (1, -1), (-1, 1)],
    [(0, 0), (1, 0), (-1, 0), (0, 1), (0, -1)],
]


def get_exp(x, dz, dy):
    pairs = [
        (((z + dz) % 4) * 4 + (y + dy) % 4, z * 4 + y) for z in range(4) for y in range(4)
    ]
    return lax.ppermute(x, "exp", pairs)


def get_x(v, dx):
    pairs = [(((x + dx) % 4) * 2 + c, x * 2 + c) for x in range(4) for c in range(2)]
    return lax.ppermute(v, "grp", pairs)


def get_core(v):
    pairs = [(x * 2 + 1 - c, x * 2 + c) for x in range(4) for c in range(2)]
    return lax.ppermute(v, "grp", pairs)


def gather_weights(gate, up, down):
    mid = gate.shape[0] // 2
    own = [
        jnp.concatenate([gate, up[:mid]], axis=0),
        jnp.concatenate([up[mid:], down], axis=0),
    ]
    right, left = [None, None], [None, None]
    for i in (0, 1):
        right[i] = get_x(own[i], 1)
        left[i] = get_x(own[i], -1)
    far = []
    for i, near in enumerate((right[0], left[1])):
        far.append(get_x(near, 1 - 2 * i))
    mine = own + right + left + far
    other = []
    for v in mine:
        other.append(get_core(v))
    return mine + other


def take(parts, row, rows):
    at = 0
    for part in parts:
        size = part.shape[0]
        if at <= row and row + rows <= at + size:
            return part if size == rows else part[row - at : row - at + rows]
        at += size
    raise ValueError("part")


def gather_tokens(t):
    blocks = {(0, 0): [t]}
    for offset, parts in TREE.items():
        blocks[offset] = []
        for row, rows, way, before in parts:
            source = take(blocks[before], row, rows)
            blocks[offset].append(get_exp(source, *way))
    return blocks


def add_up(value, extra):
    rows = value.shape[0]
    total = value.astype(jnp.float32)
    for row, v in extra:
        below = rows - row - v.shape[0]
        if row or below:
            v = jnp.pad(v, ((row, below), (0, 0)))
        total = total + v.astype(jnp.float32)
    return total.astype(jnp.bfloat16)


def reduce_back(partial):
    extra = {offset: [] for offset in partial}
    for offset, parts in reversed(BACK.items()):
        values = partial[offset]
        if extra[offset]:
            values = [add_up(values[0], extra[offset])]
        for i, (row, rows, way, before) in enumerate(parts):
            extra[before].append((row, get_exp(values[i], -way[0], -way[1])))
    return add_up(partial[0, 0][0], extra[0, 0])


def weight_pieces(n):
    half = 3 * n // 2
    pieces = []

    def cut(operand, row, kind, to, count):
        while count:
            part = min(count, NTILE - to % NTILE)
            pieces.append((operand, row, kind, to, part))
            row, to, count = row + part, to + part, count - part

    for shard in range(8):
        for kind in range(3):
            lo, hi = kind * n, (kind + 1) * n
            for part in range(2):
                start = part * half
                a, b = max(lo, start), min(hi, start + half)
                if a < b:
                    cut(2 * shard + part, a - start, kind, shard * n + a - lo, b - a)
    pieces.sort(key=lambda p: (p[2] == 2, p[3]))
    return pieces


def expert_body(nb, parts, out_parts, pieces, src_ref, meta_ref, *refs):
    weights, refs = refs[:16], refs[16:]
    inputs, refs = refs[: len(parts)], refs[len(parts) :]
    outs, refs = refs[: len(out_parts)], refs[len(out_parts) :]
    w_ref, t_ref, x_ref, h_ref, o_ref, p_ref, s_ref, k_ref, t_sem, w_sem, o_sem = refs
    hidden = w_ref.shape[1]
    width = w_ref.shape[2]
    tiles = hidden // NTILE

    for i, (b, row, rows) in enumerate(parts):
        pltpu.make_async_copy(inputs[i], t_ref.at[b, pl.ds(row, rows)], t_sem.at[b]).start()

    def fetch(stage):
        for operand, row, kind, to, count in pieces:
            if (tiles if kind == 2 else to // NTILE) == stage:
                pltpu.make_async_copy(
                    weights[operand].at[pl.ds(row, count)],
                    w_ref.at[kind, pl.ds(to, count)],
                    w_sem.at[stage],
                ).start()

    fetch(0)

    def out_copy(i):
        b, row, rows = out_parts[i]
        return pltpu.make_async_copy(p_ref.at[b, pl.ds(row, rows)], outs[i], o_sem.at[i])

    slots = lax.broadcasted_iota(jnp.int32, (CAP, 128), 0).astype(jnp.float32) + 1.0

    @pl.loop(0, nb)
    def _(b):
        source = src_ref[b]
        hit = jnp.where(slots == meta_ref[source, 0:1, :], 1.0, 0.0)
        scale = jnp.sum(hit * meta_ref[source, 1:2, :], axis=1, keepdims=True)
        rows = pl.ds(pl.multiple_of(b * CAP, CAP), CAP)
        k_ref[rows, :] = jnp.broadcast_to(scale, (CAP, 128))
        s_ref[b] = hit.T.astype(jnp.bfloat16)
        pltpu.make_async_copy(t_ref.at[b], t_ref.at[b], t_sem.at[b]).wait()
        x_ref[rows, :] = jnp.dot(
            hit.astype(jnp.bfloat16), t_ref[b], preferred_element_type=jnp.float32
        ).astype(jnp.bfloat16)

    fetch(1)

    nt = (((1,), (1,)), ((), ()))

    @pl.loop(0, tiles)
    def _(n):
        rows = pl.ds(pl.multiple_of(n * NTILE, NTILE), NTILE)
        both = w_ref.at[pl.ds(0, 2), rows]
        pltpu.make_async_copy(both, both, w_sem.at[n]).wait()
        for stage in range(2, tiles + 1):

            @pl.when(n == stage - 2)
            def _():
                fetch(stage)

        gate = lax.dot_general(x_ref[...], w_ref[0, rows, :], nt, preferred_element_type=jnp.float32)
        up = lax.dot_general(x_ref[...], w_ref[1, rows, :], nt, preferred_element_type=jnp.float32)
        h_ref[:, rows] = (gate / (1.0 + jnp.exp(-gate)) * up).astype(jnp.bfloat16)

    pltpu.make_async_copy(w_ref.at[2], w_ref.at[2], w_sem.at[tiles]).wait()

    @pl.loop(0, width // CTILE)
    def _(c):
        cols = pl.ds(pl.multiple_of(c * CTILE, CTILE), CTILE)
        out = jnp.dot(h_ref[...], w_ref[2, :, cols], preferred_element_type=jnp.float32)
        o_ref[:, cols] = (out * jnp.tile(k_ref[...], (1, CTILE // 128))).astype(jnp.bfloat16)

    @pl.loop(0, nb)
    def _(b):
        rows = pl.ds(pl.multiple_of(b * CAP, CAP), CAP)
        p_ref[b] = jnp.dot(
            s_ref[b], o_ref[rows, :], preferred_element_type=jnp.float32
        ).astype(jnp.bfloat16)
        for i, part in enumerate(out_parts):

            @pl.when(b == part[0])
            def _():
                out_copy(i).start()

    for i in range(len(out_parts)):
        out_copy(i).wait()


def expert_blocks(src, meta, blocks, weights, cuts):
    nb = len(blocks)
    parts, inputs = [], []
    for b, block in enumerate(blocks):
        row = 0
        for part in block:
            parts.append((b, row, part.shape[0]))
            inputs.append(part)
            row += part.shape[0]
    rows, width = row, inputs[0].shape[1]
    out_parts = [(b, row, size) for b, cut in enumerate(cuts) for row, size in cut]
    n = 2 * weights[0].shape[0] // 3
    hidden = 8 * n
    pieces = weight_pieces(n)
    m = nb * CAP
    anywhere = pl.BlockSpec(memory_space=pl.ANY)
    flops = 2 * m * width * hidden * 3 + 4 * m * rows * width
    moved = 2 * (3 * hidden * width + 2 * nb * rows * width)
    outs = pl.pallas_call(
        functools.partial(expert_body, nb, parts, out_parts, pieces),
        out_shape=[jax.ShapeDtypeStruct((part[2], width), jnp.bfloat16) for part in out_parts],
        in_specs=[
            pl.BlockSpec(memory_space=pltpu.SMEM),
            pl.BlockSpec(memory_space=pltpu.VMEM),
        ]
        + [anywhere] * (16 + len(parts)),
        out_specs=[anywhere] * len(out_parts),
        scratch_shapes=[
            pltpu.VMEM((3, hidden, width), jnp.bfloat16),
            pltpu.VMEM((nb, rows, width), jnp.bfloat16),
            pltpu.VMEM((m, width), jnp.bfloat16),
            pltpu.VMEM((m, hidden), jnp.bfloat16),
            pltpu.VMEM((m, width), jnp.bfloat16),
            pltpu.VMEM((nb, rows, width), jnp.bfloat16),
            pltpu.VMEM((nb, rows, CAP), jnp.bfloat16),
            pltpu.VMEM((m, 128), jnp.float32),
            pltpu.SemaphoreType.DMA((nb,)),
            pltpu.SemaphoreType.DMA((hidden // NTILE + 1,)),
            pltpu.SemaphoreType.DMA((len(out_parts),)),
        ],
        compiler_params=pltpu.CompilerParams(vmem_limit_bytes=(26 + 4 * nb) << 20),
        cost_estimate=pl.CostEstimate(flops=flops, bytes_accessed=moved, transcendentals=m * hidden),
    )(src, meta, *weights, *inputs)
    return [[v for v, part in zip(outs, out_parts) if part[0] == b] for b in range(nb)]


def per_device(tokens, expert_ids, gate_fixed, w_gate, w_up, w_down):
    me = lax.axis_index("exp")
    blocks = gather_tokens(tokens)
    weights = gather_weights(w_gate[0].T, w_up[0].T, w_down[0])

    hit = expert_ids.T[None] == jnp.arange(EXPERTS, dtype=jnp.int32)[:, None, None]
    routed = jnp.any(hit, axis=1).astype(jnp.int32)
    place = jnp.cumsum(routed, axis=1) * routed
    gate = jnp.sum(jnp.where(hit, gate_fixed.T[None], 0), axis=1)
    meta = jnp.stack([place.astype(jnp.float32), gate.astype(jnp.float32) / 65536.0], axis=1)
    meta = lax.all_to_all(meta, "exp", split_axis=0, concat_axis=0, tiled=True)

    partial = {}
    for batch in BATCHES:
        dz = jnp.array([o[0] for o in batch], jnp.int32)
        dy = jnp.array([o[1] for o in batch], jnp.int32)
        src = (((me >> 2) + dz) & 3) * 4 + ((me + dy) & 3)
        cuts = [[part[:2] for part in BACK.get(o, [(0, 128)])] for o in batch]
        outs = expert_blocks(src, meta, [blocks[o] for o in batch], weights, cuts)
        partial.update(zip(batch, outs))
    return reduce_back(partial)


def solution(mesh):
    in_specs = (
        P(("grp", "exp"), None),
        P(("grp", "exp"), None),
        P(("grp", "exp"), None),
        P("exp", None, "grp"),
        P("exp", None, "grp"),
        P("exp", "grp", None),
    )
    out_specs = P(("grp", "exp"), None)

    return jax.shard_map(
        per_device, mesh=mesh, in_specs=in_specs, out_specs=out_specs, check_vma=False
    )
```

```python
import functools

import jax
import jax.numpy as jnp
from jax import lax
from jax.experimental import pallas as pl
from jax.experimental.pallas import tpu as pltpu
from jax.sharding import PartitionSpec as P


EXPERTS = 16
CAP = 80
NTILE = 256
CTILE = 1024


TREE = {
    (1, 0): [(0, 128, (1, 0), (0, 0))],
    (-1, 0): [(0, 128, (-1, 0), (0, 0))],
    (0, 1): [(0, 128, (0, 1), (0, 0))],
    (0, -1): [(0, 128, (0, -1), (0, 0))],
    (-1, -1): [(0, 64, (-1, 0), (0, -1)), (64, 64, (-1, 0), (0, -1))],
    (1, -1): [(0, 128, (0, -1), (1, 0))],
    (-1, 1): [(0, 128, (0, 1), (-1, 0))],
    (1, 1): [(0, 128, (1, 0), (0, 1))],
    (2, -1): [(0, 64, (-1, 0), (-1, -1)), (64, 64, (-1, 0), (-1, -1))],
    (-1, 2): [(0, 64, (0, -1), (-1, -1)), (64, 64, (0, -1), (-1, -1))],
    (0, 2): [(0, 128, (0, 1), (0, 1))],
    (2, 0): [(0, 128, (1, 0), (1, 0))],
    (2, 2): [(0, 64, (0, -1), (2, -1)), (64, 64, (-1, 0), (-1, 2))],
    (1, 2): [(0, 128, (0, 1), (1, 1))],
    (2, 1): [(0, 128, (1, 0), (1, 1))],
}

BACK = {o: [(0, 128) + parts[0][2:]] for o, parts in TREE.items()}
for split in ((2, 2), (2, -1), (-1, 2), (-1, -1)):
    BACK[split] = TREE[split]

BATCHES = [
    [(2, 2), (2, 1), (1, 2)],
    [(2, -1), (-1, 2), (1, 1), (0, 2)],
    [(-1, -1), (2, 0), (1, -1), (-1, 1)],
    [(0, 0), (1, 0), (-1, 0), (0, 1), (0, -1)],
]


def get_exp(x, dz, dy):
    pairs = [
        (((z + dz) % 4) * 4 + (y + dy) % 4, z * 4 + y) for z in range(4) for y in range(4)
    ]
    return lax.ppermute(x, "exp", pairs)


def get_x(v, dx):
    pairs = [(((x + dx) % 4) * 2 + c, x * 2 + c) for x in range(4) for c in range(2)]
    return lax.ppermute(v, "grp", pairs)


def get_core(v):
    pairs = [(x * 2 + 1 - c, x * 2 + c) for x in range(4) for c in range(2)]
    return lax.ppermute(v, "grp", pairs)


def gather_weights(gate, up, down):
    mid = gate.shape[0] // 2
    own = [
        jnp.concatenate([gate, up[:mid]], axis=0),
        jnp.concatenate([up[mid:], down], axis=0),
    ]
    right, left = [None, None], [None, None]
    for i in (0, 1):
        right[i] = get_x(own[i], 1)
        left[i] = get_x(own[i], -1)
    far = []
    for i, near in enumerate((right[0], left[1])):
        far.append(get_x(near, 1 - 2 * i))
    mine = own + right + left + far
    other = []
    for v in mine:
        other.append(get_core(v))
    return mine + other


def take(parts, row, rows):
    at = 0
    for part in parts:
        size = part.shape[0]
        if at <= row and row + rows <= at + size:
            return part if size == rows else part[row - at : row - at + rows]
        at += size
    raise ValueError("part")


def gather_tokens(t):
    blocks = {(0, 0): [t]}
    for offset, parts in TREE.items():
        blocks[offset] = []
        for row, rows, way, before in parts:
            source = take(blocks[before], row, rows)
            blocks[offset].append(get_exp(source, *way))
    return blocks


def add_up(value, extra):
    rows = value.shape[0]
    total = value.astype(jnp.float32)
    for row, v in extra:
        below = rows - row - v.shape[0]
        if row or below:
            v = jnp.pad(v, ((row, below), (0, 0)))
        total = total + v.astype(jnp.float32)
    return total.astype(jnp.bfloat16)


def reduce_back(partial):
    extra = {offset: [] for offset in partial}
    for offset, parts in reversed(BACK.items()):
        for i, (row, rows, way, before) in enumerate(parts):
            value = partial[offset][i]
            mine = [
                (at - row, v)
                for at, v in extra[offset]
                if at < row + rows and row < at + v.shape[0]
            ]
            assert all(at >= 0 and at + v.shape[0] <= rows for at, v in mine)
            if mine:
                value = add_up(value, mine)
            extra[before].append((row, get_exp(value, -way[0], -way[1])))
    return add_up(partial[0, 0][0], extra[0, 0])


def weight_pieces(n):
    half = 3 * n // 2
    pieces = []

    def cut(operand, row, kind, to, count):
        while count:
            part = min(count, NTILE - to % NTILE)
            pieces.append((operand, row, kind, to, part))
            row, to, count = row + part, to + part, count - part

    for shard in range(8):
        for kind in range(3):
            lo, hi = kind * n, (kind + 1) * n
            for part in range(2):
                start = part * half
                a, b = max(lo, start), min(hi, start + half)
                if a < b:
                    cut(2 * shard + part, a - start, kind, shard * n + a - lo, b - a)
    pieces.sort(key=lambda p: (p[2] == 2, p[3]))
    return pieces


def expert_body(base, nb, parts, out_parts, pieces, src_ref, meta_ref, *refs):
    weights, refs = refs[:16], refs[16:]
    inputs, refs = refs[: len(parts)], refs[len(parts) :]
    outs, refs = refs[: len(out_parts)], refs[len(out_parts) :]
    w_ref, t_ref, x_ref, h_ref, o_ref, p_ref, s_ref, k_ref, t_sem, w_sem, o_sem = refs
    hidden = w_ref.shape[1]
    width = w_ref.shape[2]
    tiles = hidden // NTILE

    for i, (b, row, rows) in enumerate(parts):
        pltpu.make_async_copy(inputs[i], t_ref.at[b, pl.ds(row, rows)], t_sem.at[b]).start()

    def fetch(stage):
        for operand, row, kind, to, count in pieces:
            if (tiles if kind == 2 else to // NTILE) == stage:
                pltpu.make_async_copy(
                    weights[operand].at[pl.ds(row, count)],
                    w_ref.at[kind, pl.ds(to, count)],
                    w_sem.at[stage],
                ).start()

    fetch(0)

    def out_copy(i):
        b, row, rows = out_parts[i]
        return pltpu.make_async_copy(p_ref.at[b, pl.ds(row, rows)], outs[i], o_sem.at[i])

    slots = lax.broadcasted_iota(jnp.int32, (CAP, 128), 0).astype(jnp.float32) + 1.0

    @pl.loop(0, nb)
    def _(b):
        source = src_ref[base + b]
        hit = jnp.where(slots == meta_ref[source, 0:1, :], 1.0, 0.0)
        scale = jnp.sum(hit * meta_ref[source, 1:2, :], axis=1, keepdims=True)
        rows = pl.ds(pl.multiple_of(b * CAP, CAP), CAP)
        k_ref[rows, :] = jnp.broadcast_to(scale, (CAP, 128))
        s_ref[b] = hit.T.astype(jnp.bfloat16)
        pltpu.make_async_copy(t_ref.at[b], t_ref.at[b], t_sem.at[b]).wait()
        x_ref[rows, :] = jnp.dot(
            hit.astype(jnp.bfloat16), t_ref[b], preferred_element_type=jnp.float32
        ).astype(jnp.bfloat16)

    fetch(1)

    nt = (((1,), (1,)), ((), ()))

    @pl.loop(0, tiles)
    def _(n):
        rows = pl.ds(pl.multiple_of(n * NTILE, NTILE), NTILE)
        both = w_ref.at[pl.ds(0, 2), rows]
        pltpu.make_async_copy(both, both, w_sem.at[n]).wait()
        for stage in range(2, tiles + 1):

            @pl.when(n == stage - 2)
            def _():
                fetch(stage)

        gate = lax.dot_general(x_ref[...], w_ref[0, rows, :], nt, preferred_element_type=jnp.float32)
        up = lax.dot_general(x_ref[...], w_ref[1, rows, :], nt, preferred_element_type=jnp.float32)
        h_ref[:, rows] = (gate / (1.0 + jnp.exp(-gate)) * up).astype(jnp.bfloat16)

    pltpu.make_async_copy(w_ref.at[2], w_ref.at[2], w_sem.at[tiles]).wait()

    @pl.loop(0, width // CTILE)
    def _(c):
        cols = pl.ds(pl.multiple_of(c * CTILE, CTILE), CTILE)
        out = jnp.dot(h_ref[...], w_ref[2, :, cols], preferred_element_type=jnp.float32)
        o_ref[:, cols] = (out * jnp.tile(k_ref[...], (1, CTILE // 128))).astype(jnp.bfloat16)

    @pl.loop(0, nb)
    def _(b):
        rows = pl.ds(pl.multiple_of(b * CAP, CAP), CAP)
        p_ref[b] = jnp.dot(
            s_ref[b], o_ref[rows, :], preferred_element_type=jnp.float32
        ).astype(jnp.bfloat16)
        for i, part in enumerate(out_parts):

            @pl.when(b == part[0])
            def _():
                out_copy(i).start()

    for i in range(len(out_parts)):
        out_copy(i).wait()


def expert_blocks(src, base, meta, blocks, weights, cuts):
    nb = len(blocks)
    parts, inputs = [], []
    for b, block in enumerate(blocks):
        row = 0
        for part in block:
            parts.append((b, row, part.shape[0]))
            inputs.append(part)
            row += part.shape[0]
    rows, width = row, inputs[0].shape[1]
    out_parts = [(b, row, size) for b, cut in enumerate(cuts) for row, size in cut]
    n = 2 * weights[0].shape[0] // 3
    hidden = 8 * n
    pieces = weight_pieces(n)
    m = nb * CAP
    anywhere = pl.BlockSpec(memory_space=pl.ANY)
    flops = 2 * m * width * hidden * 3 + 4 * m * rows * width
    moved = 2 * (3 * hidden * width + 2 * nb * rows * width)
    outs = pl.pallas_call(
        functools.partial(expert_body, base, nb, parts, out_parts, pieces),
        out_shape=[jax.ShapeDtypeStruct((part[2], width), jnp.bfloat16) for part in out_parts],
        in_specs=[
            pl.BlockSpec(memory_space=pltpu.SMEM),
            pl.BlockSpec(memory_space=pltpu.VMEM),
        ]
        + [anywhere] * (16 + len(parts)),
        out_specs=[anywhere] * len(out_parts),
        scratch_shapes=[
            pltpu.VMEM((3, hidden, width), jnp.bfloat16),
            pltpu.VMEM((nb, rows, width), jnp.bfloat16),
            pltpu.VMEM((m, width), jnp.bfloat16),
            pltpu.VMEM((m, hidden), jnp.bfloat16),
            pltpu.VMEM((m, width), jnp.bfloat16),
            pltpu.VMEM((nb, rows, width), jnp.bfloat16),
            pltpu.VMEM((nb, rows, CAP), jnp.bfloat16),
            pltpu.VMEM((m, 128), jnp.float32),
            pltpu.SemaphoreType.DMA((nb,)),
            pltpu.SemaphoreType.DMA((hidden // NTILE + 1,)),
            pltpu.SemaphoreType.DMA((len(out_parts),)),
        ],
        compiler_params=pltpu.CompilerParams(vmem_limit_bytes=(26 + 4 * nb) << 20),
        cost_estimate=pl.CostEstimate(flops=flops, bytes_accessed=moved, transcendentals=m * hidden),
    )(src, meta, *weights, *inputs)
    return [[v for v, part in zip(outs, out_parts) if part[0] == b] for b in range(nb)]


def per_device(tokens, expert_ids, gate_fixed, w_gate, w_up, w_down):
    me = lax.axis_index("exp")
    blocks = gather_tokens(tokens)
    weights = gather_weights(w_gate[0].T, w_up[0].T, w_down[0])

    hit = expert_ids.T[None] == jnp.arange(EXPERTS, dtype=jnp.int32)[:, None, None]
    routed = jnp.any(hit, axis=1).astype(jnp.int32)
    place = jnp.cumsum(routed, axis=1) * routed
    gate = jnp.sum(jnp.where(hit, gate_fixed.T[None], 0), axis=1)
    meta = jnp.stack([place.astype(jnp.float32), gate.astype(jnp.float32) / 65536.0], axis=1)
    meta = lax.all_to_all(meta, "exp", split_axis=0, concat_axis=0, tiled=True)

    partial = {}
    dz = jnp.array([o[0] for batch in BATCHES for o in batch], jnp.int32)
    dy = jnp.array([o[1] for batch in BATCHES for o in batch], jnp.int32)
    src = (((me >> 2) + dz) & 3) * 4 + ((me + dy) & 3)
    base = 0
    for batch in BATCHES:
        cuts = [[part[:2] for part in BACK.get(o, [(0, 128)])] for o in batch]
        outs = expert_blocks(src, base, meta, [blocks[o] for o in batch], weights, cuts)
        partial.update(zip(batch, outs))
        base += len(batch)
    return reduce_back(partial)


def solution(mesh):
    in_specs = (
        P(("grp", "exp"), None),
        P(("grp", "exp"), None),
        P(("grp", "exp"), None),
        P("exp", None, "grp"),
        P("exp", None, "grp"),
        P("exp", "grp", None),
    )
    out_specs = P(("grp", "exp"), None)

    return jax.shard_map(
        per_device, mesh=mesh, in_specs=in_specs, out_specs=out_specs, check_vma=False
    )
```
